512 devices in a mesh: dp: 8 (over y, core), expert: 64 (over x, z).
Axes of the slice: x: 4, y: 4, z: 16, core: 2. Of those that a mesh axis runs over, the one named last changes fastest.
Arguments:
- tokens: bfloat16 [16384, 1024], P('expert', 'dp'), may hold values from -6 to 6
- cotangent: bfloat16 [16384, 1024], P('expert', 'dp'), may hold values from -6 to 6
- expert_ids: int32 [16384, 2], P('expert'), may hold values from 0 to 63, all different within a row; in each aligned block of 256 rows (0 to 255, 256 to 511, ...) at most 12 rows name the same one
- gate_weights: float32 [16384, 2], P('expert'), may hold values from 0.2 to 1
- weight_in: bfloat16 [64, 1024, 4096], P('expert', None, 'dp'), may hold values from -0.1875 to 0.1875
- weight_out: bfloat16 [64, 4096, 1024], P('expert', 'dp'), may hold values from -0.09375 to 0.09375
Outputs:
- output: bfloat16 [16384, 1024], P('expert', 'dp')
- grad_tokens: bfloat16 [16384, 1024], P('expert', 'dp')
- grad_weight_in: bfloat16 [64, 1024, 4096], P('expert', None, 'dp')
- grad_weight_out: bfloat16 [64, 4096, 1024], P('expert', 'dp')
The draws below stay inside these ranges and needn't reach their ends.
Inputs may be any that keep to these rules, and one draw needn't show every extreme that they name: `expert_ids`: the two experts of a token differ. In each aligned block of 256 rows (the rows of one device along expert) no expert is named by more than 12 rows, a bound that some block reaches.
All inputs are finite; a program needn't handle non-finite values.
Results may differ from the reference program's by a relative error of at most 0.015.
Values may be sent and summed in bfloat16 or wider, within the bound.
No kernel may reach another device: no remote copies, remote signals or barrier semaphores. Data moves between devices by JAX's collectives and lax.ppermute only.
A program may use at most 64 MiB of HBM per device.

```python
import math
import jax
import jax.numpy as jnp
import numpy as np
from jax import lax

D = 1024
FF = 4096
TOK_DEV = 256
EXPERTS = 64
CAP = 12
TOKENS = 16384
N_DP = 8


def shard_levels(key, extent, cuts, smallest, top_value):
    def one(dim, blocks):
        steps = jax.random.uniform(jax.random.fold_in(jax.random.fold_in(key, 6), dim), (blocks,), jnp.float32, smallest / len(cuts), top_value / len(cuts))
        return jnp.repeat(jnp.exp(steps), extent[dim] // blocks).reshape((-1,) + (1,) * (len(extent) - dim - 1))

    gain = one(*cuts[0])
    for cut in cuts[1:]:
        gain = gain * one(*cut)
    return gain


def deal_out(key, own, number, rows, number_of, top, reach, lean):
    order = jax.random.permutation(key, number_of)
    crowded, usual = portions_of(number_of, rows * top, reach, lean, True), portions_of(number_of, rows * top, reach, lean, False)
    places = jnp.arange(number_of)

    def named(tallies, rotation):
        used = int((tallies > 0).sum())
        fixed = max(1, used // 4)
        moved = fixed + (places - fixed + rotation * (used - fixed)) % max(1, number_of - fixed)
        return jnp.zeros((number_of,), jnp.int32).at[order[jnp.where(places < fixed, places, moved)]].set(jnp.asarray(tallies, jnp.int32))

    tallies = jnp.where(number % 4 == 0, named(crowded, number // 4), named(usual, number - number // 4 - 1))
    mixed = jax.random.permutation(jax.random.fold_in(own, 3), number_of)
    source_of, sink = mixed[0:number_of // 2 * 2:2], mixed[1:number_of // 2 * 2:2]
    room = jnp.minimum(tallies[source_of] - 1, reach - tallies[sink]) // 2
    room = jnp.where((source_of == order[0]) | (sink == order[0]) | (tallies[sink] == 0), 0, jnp.maximum(room, 0))
    moved = jax.random.randint(jax.random.fold_in(own, 4), (number_of // 2,), 0, 1 << 20) % (room + 1)
    tallies = tallies.at[source_of].add(-moved).at[sink].add(moved)
    members = jnp.searchsorted(jnp.cumsum(tallies), jnp.arange(rows * top), side="right").astype(jnp.int32)
    grid = members.reshape(top, rows).T
    grid = grid[jax.random.permutation(jax.random.fold_in(own, 1), rows)]
    rotation = jax.random.randint(jax.random.fold_in(own, 2), (rows, 1), 0, top)
    return jnp.take_along_axis(grid, (jnp.arange(top)[None, :] + rotation) % top, axis=1)


def portions_of(count, total, bound, skew, full):
    portions = [(1 << 20) // math.isqrt(standing ** skew) + 1 for standing in range(1, count + 1)]
    largest = bound if full else min(bound, max(-(-total // count), total * portions[0] // sum(portions)))
    least = 1 if total - largest >= count - 1 else 0
    given, rest = [largest] + [least] * (count - 1), total - largest - least * (count - 1)
    while rest > 0:
        movable = [i for i in range(1, count) if given[i] < largest] or [i for i in range(1, count) if given[i] < bound]
        mass, left = sum([portions[i] for i in movable]), rest
        for i in movable:
            more = min(bound - given[i], max(1, left * portions[i] // mass), rest)
            given[i] = given[i] + more
            rest = rest - more
    return np.array(given)


def noise(rng, extent, spread, bound, split=(), kind=jnp.bfloat16):
    level = shard_levels(rng, extent, split, -0.22, 0.18) if split else 1.0
    entries = jax.random.normal(rng, extent, jnp.float32) * spread * level
    return jnp.minimum(jnp.maximum(entries, -bound), bound).astype(kind)


def setup_inputs(seed: int = 0) -> dict:
    key_of = jax.random.split(jax.random.key(seed), 7)
    tokens = noise(key_of[0], (TOKENS, D), 1.0, 6.0, ((0, 64), (1, 8)))
    cotangent = noise(key_of[1], (TOKENS, D), 1.0, 6.0, ((0, 64), (1, 8)))
    expert_ids_keys = jax.random.split(jax.random.fold_in(key_of[2], 1), TOKENS // TOK_DEV)
    expert_ids_turns = jax.random.permutation(jax.random.fold_in(key_of[2], 3), TOKENS // TOK_DEV)
    expert_ids = jax.vmap(lambda own, number: deal_out(jax.random.fold_in(key_of[2], 2), own, number, TOK_DEV, EXPERTS, 2, CAP, 2))(expert_ids_keys, expert_ids_turns).reshape((TOKENS, 2))
    gate_weights = jnp.clip(0.2 + 0.8 * jax.random.uniform(key_of[3], (TOKENS, 2), jnp.float32) ** shard_levels(key_of[3], (TOKENS, 2), ((0, 64),), -0.2, 0.2), 0.2, 1.0)
    weight_in = noise(key_of[4], (EXPERTS, D, FF), D ** -0.5, 0.1875, ((0, 64), (2, 8)))
    weight_out = noise(key_of[5], (EXPERTS, FF, D), FF ** -0.5, 0.09375, ((0, 64), (1, 8)))
    return dict(tokens=tokens, cotangent=cotangent, expert_ids=expert_ids, gate_weights=gate_weights, weight_in=weight_in, weight_out=weight_out)


half_root = 0.7071067811865476
inv_root_tau = 0.3989422804014327


def gelu_exact(value):
    return 0.5 * value * (1.0 + jax.scipy.special.erf(value * half_root))


def gelu_slope(value):
    return 0.5 * (1.0 + jax.scipy.special.erf(value * half_root)) + value * inv_root_tau * jnp.exp(-0.5 * value * value)


def slot_owner(block_ids, capacity, experts):
    flat_ids = block_ids.reshape(-1).astype(jnp.int32)
    count = flat_ids.shape[0]
    onehot = (flat_ids[:, None] == jnp.arange(experts, dtype=jnp.int32)[None, :]).astype(jnp.int32)
    position = (jnp.sum(jnp.cumsum(onehot, axis=0) * onehot, axis=1) - 1).astype(jnp.int32)
    slot_index = (flat_ids * capacity + position).astype(jnp.int32)
    owner_of = jnp.full((experts * capacity,), -1, jnp.int32).at[slot_index].set(jnp.arange(count, dtype=jnp.int32))
    return slot_index, owner_of


def round_then_sum(values):
    rounded = lax.optimization_barrier(values.astype(jnp.bfloat16))
    return jnp.sum(rounded.astype(jnp.float32), axis=1)


def expert_work(inputs, scaled, weight_in, weight_out):
    rows = inputs.shape[0]
    width = FF // N_DP
    pre_act = jnp.dot(inputs, weight_in, preferred_element_type=jnp.float32)
    hidden = gelu_exact(pre_act).astype(jnp.bfloat16)
    parted = jnp.einsum("rnf,nfd->rnd", hidden.reshape(rows, N_DP, width).astype(jnp.float32),
                        weight_out.reshape(N_DP, width, D).astype(jnp.float32))
    out_rows = round_then_sum(parted)
    grad_hidden = jnp.dot(scaled, weight_out.T, preferred_element_type=jnp.float32)
    d_pre = (grad_hidden * gelu_slope(pre_act)).astype(jnp.bfloat16)
    backed = jnp.einsum("rnf,dnf->rnd", d_pre.reshape(rows, N_DP, width).astype(jnp.float32),
                        weight_in.reshape(D, N_DP, width).astype(jnp.float32))
    back_rows = round_then_sum(backed)
    grad_out = jnp.dot(hidden.T, scaled, preferred_element_type=jnp.float32).astype(jnp.bfloat16)
    grad_in = jnp.dot(inputs.T, d_pre, preferred_element_type=jnp.float32).astype(jnp.bfloat16)
    return out_rows, back_rows, grad_in, grad_out


def reference(tokens, cotangent, expert_ids, gate_weights, weight_in, weight_out):
    blocks = TOKENS // TOK_DEV
    scaled_all = (gate_weights[:, :, None] * cotangent[:, None, :].astype(jnp.float32)).astype(jnp.bfloat16).reshape(2 * TOKENS, D)
    gate_flat = gate_weights.reshape(-1)
    slots, owners = jax.vmap(lambda block: slot_owner(block, CAP, EXPERTS))(expert_ids.reshape(blocks, TOK_DEV, 2))
    base = (jnp.arange(blocks, dtype=jnp.int32) * (2 * TOK_DEV))[:, None]
    global_owner = jnp.where(owners >= 0, owners + base, -1).astype(jnp.int32).reshape(blocks, EXPERTS, CAP)

    def per_expert(carry, index):
        out_sum, back_sum = carry
        owner_rows = lax.dynamic_index_in_dim(global_owner, index, axis=1, keepdims=False).reshape(-1)
        filled = owner_rows >= 0
        safe_owner = jnp.maximum(owner_rows, 0).astype(jnp.int32)
        token_rows = (safe_owner // 2).astype(jnp.int32)
        inputs = jnp.where(filled[:, None], tokens[token_rows], jnp.zeros((), jnp.bfloat16))
        scaled = jnp.where(filled[:, None], scaled_all[safe_owner], jnp.zeros((), jnp.bfloat16))
        expert_in = lax.dynamic_index_in_dim(weight_in, index, 0, keepdims=False)
        expert_out = lax.dynamic_index_in_dim(weight_out, index, 0, keepdims=False)
        out_rows, back_rows, grad_in, grad_out = expert_work(inputs, scaled, expert_in, expert_out)
        gates = jnp.where(filled, gate_flat[safe_owner], jnp.zeros((), gate_flat.dtype))
        target = jnp.where(filled, token_rows, TOKENS).astype(jnp.int32)
        out_sum = out_sum.at[target].add(gates[:, None] * out_rows, mode="drop")
        back_sum = back_sum.at[target].add(back_rows, mode="drop")
        return (out_sum, back_sum), (grad_in, grad_out)

    start = (jnp.zeros((TOKENS, D), jnp.float32), jnp.zeros((TOKENS, D), jnp.float32))
    (out_sum, back_sum), (grad_in, grad_out) = lax.scan(per_expert, start, jnp.arange(EXPERTS, dtype=jnp.int32))
    return out_sum.astype(jnp.bfloat16), back_sum.astype(jnp.bfloat16), grad_in, grad_out
```

```python
import jax
import jax.numpy as jnp
from jax import lax
from jax.experimental import pallas as pl
from jax.experimental.pallas import tpu as pltpu
from jax.sharding import Mesh, PartitionSpec as P

half_root = 0.7071067811865476
inv_root_tau = 0.3989422804014327

XZ = ("x", "z")
bf16 = jnp.bfloat16
f32 = jnp.float32


def dot(left, right, left_dim=1, right_dim=0):
    return lax.dot_general(
        left, right, (((left_dim,), (right_dim,)), ((), ())), preferred_element_type=f32
    )


def iota(shape, dim):
    return lax.broadcasted_iota(jnp.int32, shape, dim)


def gate_columns(gates_ref):
    rows = jnp.concatenate([gates_ref[...], jnp.zeros((6, gates_ref.shape[1]), f32)], axis=0)
    return jnp.transpose(rows)


def dispatch_kernel(ids_ref, gates_ref, tok_ref, cot_ref, send_ref, pick_ref):
    experts, _, group, _ = send_ref.shape
    rows = tok_ref.shape[0]
    ids = ids_ref[...]
    which = iota((experts, rows), 0)
    first = which == ids[0:1, :]
    second = which == ids[1:2, :]
    member = jnp.where(first | second, 1.0, 0.0).astype(bf16)
    earlier = jnp.where(iota((rows, rows), 0) < iota((rows, rows), 1), 1.0, 0.0).astype(bf16)
    rank = dot(member, earlier)
    ranks = jnp.concatenate(
        [jnp.where(first, rank, -1.0), jnp.where(second, rank, -1.0)], axis=1
    ).astype(bf16)
    slots = experts * group
    at = iota((slots, experts), 0) - group * iota((slots, experts), 1)
    owner = jnp.where((at >= 0) & (at < group), 1.0, 0.0).astype(bf16)
    spread = dot(owner, ranks)
    lane = iota((slots, 2 * rows), 0) & (group - 1)
    low = jnp.where(spread == lane.astype(f32), 1.0, 0.0).astype(bf16)
    high = jnp.where(spread == (8 + (lane & 3)).astype(f32), 1.0, 0.0).astype(bf16)
    pick_ref[0:slots, :] = low
    pick_ref[slots : 2 * slots, :] = high
    gates = gate_columns(gates_ref)
    cot = cot_ref[...].astype(f32)
    tok = tok_ref[...]
    source = jnp.concatenate(
        [
            jnp.concatenate([tok, (gates[:, 0:1] * cot).astype(bf16)], axis=1),
            jnp.concatenate([tok, (gates[:, 1:2] * cot).astype(bf16)], axis=1),
        ],
        axis=0,
    )
    width = tok.shape[1]
    chosen = dot(low, source).astype(bf16)
    rest = dot(high, source)
    mixed = jnp.where((iota((slots, width), 0) & 7) < 4, rest[:, :width], rest[:, width:])
    send_ref[:, 0] = chosen[:, :width].reshape(experts, group, width)
    send_ref[:, 1] = chosen[:, width:].reshape(experts, group, width)
    send_ref[:, 2] = mixed.astype(bf16).reshape(experts, group, width)


def dispatch(ids, gates, tokens, cotangent, experts):
    rows, width = tokens.shape
    return pl.pallas_call(
        dispatch_kernel,
        out_shape=(
            jax.ShapeDtypeStruct((experts, 3, 8, width), bf16),
            jax.ShapeDtypeStruct((experts * 16, 2 * rows), bf16),
        ),
        name="dispatch",
    )(ids.T, gates.T, tokens, cotangent)


def combine_kernel(pick_ref, gates_ref, ret_ref, out_ref, grad_ref):
    experts, _, group, width = ret_ref.shape
    rows = out_ref.shape[0]
    slots = experts * group
    tail = ret_ref[:, 2].reshape(slots, width)
    is_out = (iota((slots, width), 0) & 7) < 4
    nothing = jnp.zeros((slots, width), f32)
    tail = tail.astype(f32)
    low = jnp.concatenate(
        [ret_ref[:, 0].reshape(slots, width), ret_ref[:, 1].reshape(slots, width)], axis=1
    )
    high = jnp.concatenate(
        [jnp.where(is_out, tail, nothing), jnp.where(is_out, nothing, tail)], axis=1
    ).astype(bf16)
    both = jnp.concatenate([low, high], axis=0)
    mine = dot(pick_ref[...], both, 0, 0)
    gates = gate_columns(gates_ref)
    out_ref[...] = (
        gates[:, 0:1] * mine[:rows, :width] + gates[:, 1:2] * mine[rows:, :width]
    ).astype(bf16)
    grad_ref[...] = (mine[:rows, width:] + mine[rows:, width:]).astype(bf16)


def combine(pick, gates, ret, rows):
    width = ret.shape[-1]
    shape = jax.ShapeDtypeStruct((rows, width), bf16)
    return pl.pallas_call(combine_kernel, out_shape=(shape, shape), name="combine")(
        pick, gates.T, ret
    )


def expert_kernel(core_ref, own_ref, other_ref, win_ref, wout_ref, mine_ref, theirs_ref, x_ref, s_ref, h_ref, d_ref, tail_ref, low_ref):
    n_y, experts, _, group, width = own_ref.shape
    core = core_ref[0]
    slots = experts * group
    half = slots // 2
    for y in range(n_y):
        for ref, which in ((own_ref, core), (other_ref, 1 - core)):
            at = pl.ds(pl.multiple_of((2 * y + which) * width, width), width)
            x_ref[0:slots, at] = ref[y, :, 0].reshape(slots, width)
            s_ref[0:slots, at] = ref[y, :, 1].reshape(slots, width)
            tail_ref[:, at] = ref[y, :, 2].reshape(slots, width)
    row = iota((half, slots), 0)
    source = iota((half, slots), 1)
    base = (row >> 2) * 8 + (row & 3)
    take_in = jnp.where(source == base, 1.0, 0.0).astype(bf16)
    take_scaled = jnp.where(source == base + 4, 1.0, 0.0).astype(bf16)
    tail = tail_ref[...]
    x_ref[slots : slots + half, :] = dot(take_in, tail).astype(bf16)
    s_ref[slots : slots + half, :] = dot(take_scaled, tail).astype(bf16)
    win = win_ref[...]
    wout = wout_ref[...]
    pre = dot(x_ref[...], win)
    cdf = 0.5 * (1.0 + lax.erf(pre * half_root))
    hidden = (pre * cdf).astype(bf16)
    h_ref[...] = hidden
    slope = cdf + pre * inv_root_tau * jnp.exp(-0.5 * pre * pre)
    d_pre = (dot(s_ref[...], wout, 1, 1) * slope).astype(bf16)
    d_ref[...] = d_pre
    out = dot(hidden, wout).astype(bf16)
    back = dot(d_pre, win, 1, 1).astype(bf16)
    low_ref[0] = out[0:slots]
    low_ref[1] = back[0:slots]
    tail_ref[...] = (dot(take_in, out[slots:], 0, 0) + dot(take_scaled, back[slots:], 0, 0)).astype(bf16)
    for y in range(n_y):
        for ref, which in ((mine_ref, core), (theirs_ref, 1 - core)):
            at = pl.ds(pl.multiple_of((2 * y + which) * width, width), width)
            ref[y, :, 0] = low_ref[0, :, at].reshape(experts, group, width)
            ref[y, :, 1] = low_ref[1, :, at].reshape(experts, group, width)
            ref[y, :, 2] = tail_ref[:, at].reshape(experts, group, width)


def expert_work(core, own, other, w_in, w_out):
    n_y, experts, _, group, width = own.shape
    slots = experts * group
    rows = slots + slots // 2
    model, units = w_in.shape
    part = jax.ShapeDtypeStruct(own.shape, bf16)
    vmem = pl.BlockSpec(memory_space=pltpu.VMEM)
    return pl.pallas_call(
        expert_kernel,
        in_specs=[pl.BlockSpec(memory_space=pltpu.SMEM)] + [vmem] * 4,
        out_specs=(vmem,) * 6,
        out_shape=(
            part,
            part,
            jax.ShapeDtypeStruct((rows, model), bf16),
            jax.ShapeDtypeStruct((rows, model), bf16),
            jax.ShapeDtypeStruct((rows, units), bf16),
            jax.ShapeDtypeStruct((rows, units), bf16),
        ),
        scratch_shapes=[pltpu.VMEM((slots, model), bf16), pltpu.VMEM((2, slots, model), bf16)],
        name="expert",
    )(core, own, other, w_in, w_out)


def on_device(tokens, cotangent, expert_ids, gate_weights, weight_in, weight_out):
    experts = lax.axis_size("x") * lax.axis_size("z")
    n_y = lax.axis_size("y")
    rows, width = tokens.shape
    swap = [(0, 1), (1, 0)]
    send, pick = dispatch(expert_ids, gate_weights, tokens, cotangent, experts)
    got = lax.all_to_all(send, XZ, 0, 0, tiled=True)
    own = lax.all_to_all(jnp.broadcast_to(got[None], (n_y,) + got.shape), "y", 0, 0, tiled=True)
    other = lax.ppermute(own, "core", swap)
    core = lax.axis_index("core").astype(jnp.int32).reshape(1)
    mine, theirs, x, s, h, d = expert_work(core, own, other, weight_in[0], weight_out[0])
    pair = (mine.astype(f32) + lax.ppermute(theirs, "core", swap).astype(f32)).astype(bf16)
    parts = lax.all_to_all(pair, "y", 0, 0, tiled=True)
    summed = jnp.sum(parts.astype(f32), axis=0).astype(bf16)
    ret = lax.all_to_all(summed, XZ, 0, 0, tiled=True)
    output, grad_tokens = combine(pick, gate_weights, ret, rows)
    grad_out = dot(h, s, 0, 0).astype(bf16)
    grad_in = dot(x, d, 0, 0).astype(bf16)
    return output, grad_tokens, grad_in[None], grad_out[None]


def solution(mesh):
    cores = 2
    n_dp, n_expert = mesh.devices.shape
    n_x = 4
    grid = mesh.devices.reshape(n_dp // cores, cores, n_x, n_expert // n_x)
    fine = Mesh(grid, ("y", "core", "x", "z"))
    dp = ("y", "core")
    return jax.shard_map(
        on_device,
        mesh=fine,
        in_specs=(P(XZ, dp), P(XZ, dp), P(XZ, None), P(XZ, None), P(XZ, None, dp), P(XZ, dp, None)),
        out_specs=(P(XZ, dp), P(XZ, dp), P(XZ, None, dp), P(XZ, dp, None)),
        check_vma=False,
    )
```

```python
import jax
import jax.numpy as jnp
from jax import lax
from jax.experimental import pallas as pl
from jax.experimental.pallas import tpu as pltpu
from jax.sharding import Mesh, PartitionSpec as P

half_root = 0.7071067811865476
inv_root_tau = 0.3989422804014327

XZ = ("x", "z")
bf16 = jnp.bfloat16
f32 = jnp.float32


def dot(left, right, left_dim=1, right_dim=0):
    return lax.dot_general(
        left, right, (((left_dim,), (right_dim,)), ((), ())), preferred_element_type=f32
    )


def iota(shape, dim):
    return lax.broadcasted_iota(jnp.int32, shape, dim)


def columns(rows):
    pad = jnp.zeros((8 - rows.shape[0], rows.shape[1]), rows.dtype)
    return jnp.transpose(jnp.concatenate([rows, pad], axis=0))


def ones_where(mask):
    return jnp.where(mask, 1.0, 0.0).astype(bf16)


def fetch(pairs, sems):
    copies = [pltpu.make_async_copy(src, dst, sems.at[i]) for i, (src, dst) in enumerate(pairs)]
    for copy in copies:
        copy.start()
    return copies


def dispatch_kernel(ids_hbm, gates_hbm, tok_hbm, cot_hbm, send_ref, ids_ref, gates_ref, tok_ref, cot_ref, sems):
    copies = fetch(
        ((ids_hbm, ids_ref), (gates_hbm, gates_ref), (tok_hbm, tok_ref), (cot_hbm, cot_ref)), sems
    )
    experts, _, group, width = send_ref.shape
    rows = tok_ref.shape[0]
    slots = experts * group
    which = iota((experts, rows), 0)
    earlier = ones_where(iota((rows, rows), 0) < iota((rows, rows), 1))
    at = iota((slots, experts), 0) - group * iota((slots, experts), 1)
    owner = ones_where((at >= 0) & (at < group))
    lane = iota((slots, 2 * rows), 0) & (group - 1)
    copies[0].wait()
    ids = ids_ref[...]
    first = which == ids[0:1, :]
    second = which == ids[1:2, :]
    rank = dot(ones_where(first | second), earlier)
    ranks = jnp.concatenate(
        [jnp.where(first, rank, -1.0), jnp.where(second, rank, -1.0)], axis=1
    ).astype(bf16)
    spread = dot(owner, ranks)
    low = ones_where(spread == lane.astype(f32))
    high = ones_where(spread == (8 + (lane & 3)).astype(f32))
    for copy in copies[1:]:
        copy.wait()
    gates = columns(gates_ref[...])
    cot = cot_ref[...].astype(f32)
    tok = tok_ref[...]
    source = jnp.concatenate(
        [
            jnp.concatenate([tok, (gates[:, 0:1] * cot).astype(bf16)], axis=1),
            jnp.concatenate([tok, (gates[:, 1:2] * cot).astype(bf16)], axis=1),
        ],
        axis=0,
    )
    chosen = dot(low, source).astype(bf16)
    rest = dot(high, source)
    mixed = jnp.where((iota((slots, width), 0) & 7) < 4, rest[:, :width], rest[:, width:])
    send_ref[:, 0] = chosen[:, :width].reshape(experts, group, width)
    send_ref[:, 1] = chosen[:, width:].reshape(experts, group, width)
    send_ref[:, 2] = mixed.astype(bf16).reshape(experts, group, width)


def dispatch(ids, gates, tokens, cotangent, experts):
    rows, width = tokens.shape
    return pl.pallas_call(
        dispatch_kernel,
        in_specs=[pl.BlockSpec(memory_space=pltpu.HBM)] * 4,
        out_shape=jax.ShapeDtypeStruct((experts, 3, 8, width), bf16),
        scratch_shapes=[
            pltpu.VMEM((2, rows), jnp.int32),
            pltpu.VMEM((2, rows), f32),
            pltpu.VMEM((rows, width), bf16),
            pltpu.VMEM((rows, width), bf16),
            pltpu.SemaphoreType.DMA((4,)),
        ],
        name="dispatch",
    )(ids.T, gates.T, tokens, cotangent)


def route_kernel(ids_ref, gates_ref, pick_ref, gate_ref):
    rows = ids_ref.shape[1]
    slots = pick_ref.shape[1] // 2
    experts = slots // 8
    ids = columns(ids_ref[...])
    which = iota((rows, experts), 1)
    first = which == ids[:, 0:1]
    second = which == ids[:, 1:2]
    earlier = ones_where(iota((rows, rows), 1) < iota((rows, rows), 0))
    rank = dot(earlier, ones_where(first | second))
    ranks = jnp.concatenate(
        [jnp.where(first, rank, -1.0), jnp.where(second, rank, -1.0)], axis=0
    ).astype(bf16)
    at = iota((experts, slots), 1) - 8 * iota((experts, slots), 0)
    spread = dot(ranks, ones_where((at >= 0) & (at < 8)))
    lane = iota((2 * rows, slots), 1) & 7
    pick_ref[:, 0:slots] = ones_where(spread == lane.astype(f32))
    pick_ref[:, slots : 2 * slots] = ones_where(spread == (8 + (lane & 3)).astype(f32))
    gates = columns(gates_ref[...])
    width = gate_ref.shape[1]
    gate_ref[0:rows, :] = jnp.broadcast_to(gates[:, 0:1], (rows, width))
    gate_ref[rows : 2 * rows, :] = jnp.broadcast_to(gates[:, 1:2], (rows, width))


def route(ids, gates, experts, width):
    rows = ids.shape[0]
    return pl.pallas_call(
        route_kernel,
        out_shape=(
            jax.ShapeDtypeStruct((2 * rows, experts * 16), bf16),
            jax.ShapeDtypeStruct((2 * rows, width), f32),
        ),
        compiler_params=pltpu.CompilerParams(vmem_limit_bytes=12 << 20),
        name="route",
    )(ids.T, gates.T)


def combine_kernel(pick_ref, gate_ref, ret_ref, out_ref, grad_ref):
    experts, _, group, width = ret_ref.shape
    rows = out_ref.shape[0]
    slots = experts * group
    tail = ret_ref[:, 2].reshape(slots, width).astype(f32)
    is_out = (iota((slots, width), 0) & 7) < 4
    low = jnp.concatenate(
        [ret_ref[:, 0].reshape(slots, width), ret_ref[:, 1].reshape(slots, width)], axis=1
    )
    high = jnp.concatenate(
        [jnp.where(is_out, tail, 0.0), jnp.where(is_out, 0.0, tail)], axis=1
    ).astype(bf16)
    mine = dot(pick_ref[...], jnp.concatenate([low, high], axis=0))
    scaled = gate_ref[...] * mine[:, :width]
    out_ref[...] = (scaled[:rows] + scaled[rows:]).astype(bf16)
    grad_ref[...] = (mine[:rows, width:] + mine[rows:, width:]).astype(bf16)


def combine(pick, gate, ret, rows):
    width = ret.shape[-1]
    shape = jax.ShapeDtypeStruct((rows, width), bf16)
    return pl.pallas_call(
        combine_kernel,
        out_shape=(shape, shape),
        compiler_params=pltpu.CompilerParams(vmem_limit_bytes=12 << 20),
        name="combine",
    )(pick, gate, ret)


def half_features(ref, out_ref):
    n_y, experts, _, group, width = ref.shape
    slots = experts * group
    half = slots // 2
    row, source = iota((half, slots), 0), iota((half, slots), 1)
    base = (row >> 2) * 8 + (row & 3)
    tails = []
    for y in range(n_y):
        at = slice(y * width, (y + 1) * width)
        out_ref[0, 0:slots, at] = ref[y, :, 0].reshape(slots, width)
        out_ref[1, 0:slots, at] = ref[y, :, 1].reshape(slots, width)
        tails.append(ref[y, :, 2].reshape(slots, width))
    tail = jnp.concatenate(tails, axis=1)
    out_ref[0, slots:, :] = dot(ones_where(source == base), tail).astype(bf16)
    out_ref[1, slots:, :] = dot(ones_where(source == base + 4), tail).astype(bf16)


def of_core(y, core, width):
    return pl.ds(pl.multiple_of((2 * y + core) * width, width), width)


def weight_copies(core, win_hbm, wout_hbm, win_ref, wout_ref, sems, n_y):
    width = win_ref.shape[0] // n_y
    pairs = []
    for y in range(n_y):
        at = of_core(y, core, width)
        here = pl.ds(y * width, width)
        pairs.append((win_hbm.at[at, :], win_ref.at[here, :]))
        pairs.append((wout_hbm.at[:, at], wout_ref.at[:, here]))
    return fetch(pairs, sems)


def own_kernel(core_ref, own_ref, win_hbm, wout_hbm, feat_ref, pre_ref, win_ref, wout_ref, sems):
    copies = weight_copies(core_ref[0], win_hbm, wout_hbm, win_ref, wout_ref, sems, own_ref.shape[0])
    half_features(own_ref, feat_ref)
    for copy in copies:
        copy.wait()
    pre_ref[0] = dot(feat_ref[0], win_ref[...])
    pre_ref[1] = dot(feat_ref[1], wout_ref[...], 1, 1)


def write_part(hidden, d_pre, win, wout, ref):
    n_y, experts, _, group, width = ref.shape
    slots = experts * group
    half = slots // 2
    row, source = iota((half, slots), 0), iota((half, slots), 1)
    base = (row >> 2) * 8 + (row & 3)
    out = dot(hidden, wout).astype(bf16)
    back = dot(d_pre, win, 1, 1).astype(bf16)
    tail = dot(ones_where(source == base), out[slots:], 0, 0)
    tail = (tail + dot(ones_where(source == base + 4), back[slots:], 0, 0)).astype(bf16)
    for y in range(n_y):
        at = slice(y * width, (y + 1) * width)
        ref[y, :, 0] = out[:slots, at].reshape(experts, group, width)
        ref[y, :, 1] = back[:slots, at].reshape(experts, group, width)
        ref[y, :, 2] = tail[:, at].reshape(experts, group, width)


def main_kernel(core_ref, other_ref, pre_ref, win_hbm, wout_hbm, theirs_ref, feat_ref, act_ref, win_ref, wout_ref, sems):
    copies = weight_copies(1 - core_ref[0], win_hbm, wout_hbm, win_ref, wout_ref, sems, other_ref.shape[0])
    half_features(other_ref, feat_ref)
    for copy in copies:
        copy.wait()
    win = win_ref[...]
    wout = wout_ref[...]
    pre = pre_ref[0] + dot(feat_ref[0], win)
    cdf = 0.5 * (1.0 + lax.erf(pre * half_root))
    hidden = (pre * cdf).astype(bf16)
    act_ref[0] = hidden
    slope = cdf + pre * inv_root_tau * jnp.exp(-0.5 * pre * pre)
    d_pre = ((pre_ref[1] + dot(feat_ref[1], wout, 1, 1)) * slope).astype(bf16)
    act_ref[1] = d_pre
    write_part(hidden, d_pre, win, wout, theirs_ref)


def mine_kernel(core_ref, own_ref, other_ref, act_ref, win_hbm, wout_hbm, mine_ref, feat_ref, win_ref, wout_ref, sems):
    core = core_ref[0]
    n_y = mine_ref.shape[0]
    width = mine_ref.shape[-1]
    copies = weight_copies(core, win_hbm, wout_hbm, win_ref, wout_ref, sems, n_y)
    for y in range(n_y):
        at = slice(y * width, (y + 1) * width)
        feat_ref[:, :, of_core(y, core, width)] = own_ref[:, :, at]
        feat_ref[:, :, of_core(y, 1 - core, width)] = other_ref[:, :, at]
    for copy in copies:
        copy.wait()
    write_part(act_ref[0], act_ref[1], win_ref[...], wout_ref[...], mine_ref)


def expert_call(kernel, name, operands, results, w_in, w_out):
    model, units = w_in.shape
    vmem = pl.BlockSpec(memory_space=pltpu.VMEM)
    weights = [pltpu.with_memory_space_constraint(w, pltpu.HBM) for w in (w_in, w_out)]
    return pl.pallas_call(
        kernel,
        in_specs=[pl.BlockSpec(memory_space=pltpu.SMEM)]
        + [vmem] * (len(operands) - 1)
        + [pl.BlockSpec(memory_space=pltpu.HBM)] * 2,
        out_specs=(vmem,) * len(results) if len(results) > 1 else vmem,
        out_shape=results if len(results) > 1 else results[0],
        scratch_shapes=[
            pltpu.VMEM((model // 2, units), bf16),
            pltpu.VMEM((units, model // 2), bf16),
            pltpu.SemaphoreType.DMA((8,)),
        ],
        compiler_params=pltpu.CompilerParams(vmem_limit_bytes=24 << 20),
        name=name,
    )(*operands, *weights)


def fold_kernel(parts_ref, out_ref):
    parts = [parts_ref[y].astype(f32) for y in range(parts_ref.shape[0])]
    out_ref[...] = sum(parts[1:], parts[0]).astype(bf16)


def fold(parts):
    return pl.pallas_call(
        fold_kernel,
        out_shape=jax.ShapeDtypeStruct(parts.shape[1:], bf16),
        compiler_params=pltpu.CompilerParams(vmem_limit_bytes=12 << 20),
        name="fold",
    )(parts)


def on_device(tokens, cotangent, expert_ids, gate_weights, weight_in, weight_out):
    experts = lax.axis_size("x") * lax.axis_size("z")
    n_y = lax.axis_size("y")
    rows, width = tokens.shape
    swap = [(0, 1), (1, 0)]
    send = dispatch(expert_ids, gate_weights, tokens, cotangent, experts)
    blocks = send.shape
    got = lax.all_to_all(send.reshape(experts, -1, width), XZ, 0, 0, tiled=True)
    got = jnp.broadcast_to(got.reshape(1, -1, width), (n_y, got.size // width, width))
    own = lax.all_to_all(got, "y", 0, 0, tiled=True)
    other = lax.ppermute(own, "core", swap).reshape((n_y,) + blocks)
    own = own.reshape((n_y,) + blocks)
    core = lax.axis_index("core").astype(jnp.int32).reshape(1)
    w_in, w_out = weight_in[0], weight_out[0]
    model, units = w_in.shape
    rows_in = experts * 12
    part = jax.ShapeDtypeStruct((n_y,) + blocks, bf16)
    feat = jax.ShapeDtypeStruct((2, rows_in, model // 2), bf16)
    act = jax.ShapeDtypeStruct((2, rows_in, units), bf16)
    own_feat, pre = expert_call(
        own_kernel,
        "own",
        (core, own),
        (feat, jax.ShapeDtypeStruct((2, rows_in, units), f32)),
        w_in,
        w_out,
    )
    theirs, other_feat, acts = expert_call(
        main_kernel, "main", (core, other, pre), (part, feat, act), w_in, w_out
    )
    mine, feats = expert_call(
        mine_kernel,
        "mine",
        (core, own_feat, other_feat, acts),
        (part, jax.ShapeDtypeStruct((2, rows_in, model), bf16)),
        w_in,
        w_out,
    )
    x, s, h, d = feats[0], feats[1], acts[0], acts[1]
    mine, theirs = (p.reshape(n_y, -1, width) for p in (mine, theirs))
    pair = (mine.astype(f32) + lax.ppermute(theirs, "core", swap).astype(f32)).astype(bf16)
    summed = fold(lax.all_to_all(pair, "y", 0, 0, tiled=True)).reshape(experts, -1, width)
    summed, ids, gates = lax.optimization_barrier((summed, expert_ids, gate_weights))
    pick, gate = route(ids, gates, experts, width)
    ret = lax.all_to_all(summed, XZ, 0, 0, tiled=True).reshape(blocks)
    output, grad_tokens = combine(pick, gate, ret, rows)
    grad_out = dot(h, s, 0, 0).astype(bf16)
    grad_in = dot(x, d, 0, 0).astype(bf16)
    return output, grad_tokens, grad_in[None], grad_out[None]


def solution(mesh):
    cores = 2
    n_dp, n_expert = mesh.devices.shape
    n_x = 4
    grid = mesh.devices.reshape(n_dp // cores, cores, n_x, n_expert // n_x)
    fine = Mesh(grid, ("y", "core", "x", "z"))
    dp = ("y", "core")
    return jax.shard_map(
        on_device,
        mesh=fine,
        in_specs=(P(XZ, dp), P(XZ, dp), P(XZ, None), P(XZ, None), P(XZ, None, dp), P(XZ, dp, None)),
        out_specs=(P(XZ, dp), P(XZ, dp), P(XZ, None, dp), P(XZ, dp, None)),
        check_vma=False,
    )
```

```python
import jax
import jax.numpy as jnp
from jax import lax
from jax.experimental import pallas as pl
from jax.experimental.pallas import tpu as pltpu
from jax.sharding import Mesh, PartitionSpec as P

half_root = 0.7071067811865476
inv_root_tau = 0.3989422804014327

XZ = ("x", "z")
CXZ = ("core", "x", "z")
bf16 = jnp.bfloat16
f32 = jnp.float32

HALF = 6
CHUNK = 12


def dot(left, right, left_dim=1, right_dim=0):
    return lax.dot_general(
        left, right, (((left_dim,), (right_dim,)), ((), ())), preferred_element_type=f32
    )


def iota(shape, dim):
    return lax.broadcasted_iota(jnp.int32, shape, dim)


def columns(rows):
    pad = jnp.zeros((8 - rows.shape[0], rows.shape[1]), rows.dtype)
    return jnp.transpose(jnp.concatenate([rows, pad], axis=0))


def ones_where(mask):
    return jnp.where(mask, 1.0, 0.0).astype(bf16)


def fetch(pairs, sems):
    copies = [pltpu.make_async_copy(src, dst, sems.at[i]) for i, (src, dst) in enumerate(pairs)]
    for copy in copies:
        copy.start()
    return copies


def row_of(shape, dim, experts):
    row = iota(shape, dim)
    chunk = ((row.astype(f32) + 0.5) * (1.0 / CHUNK)).astype(jnp.int32)
    at = row - CHUNK * chunk
    core = jnp.where(chunk >= experts, 1, 0)
    group, place = at >> 2, at & 3
    mixed = group == 1
    is_input = jnp.where(mixed, place >> 1, group) == 0
    slot = HALF * core + jnp.where(mixed, 4 + (place & 1), place)
    return chunk - experts * core, slot, is_input


def dispatch_kernel(ids_hbm, gates_hbm, tok_hbm, cot_hbm, send_ref, ids_ref, gates_ref, tok_ref, cot_ref, sems):
    copies = fetch(
        ((ids_hbm, ids_ref), (gates_hbm, gates_ref), (tok_hbm, tok_ref), (cot_hbm, cot_ref)), sems
    )
    n_send, width = send_ref.shape
    experts = n_send // (2 * CHUNK)
    rows = tok_ref.shape[0]
    which = iota((experts, rows), 0)
    earlier = ones_where(iota((rows, rows), 0) < iota((rows, rows), 1))
    expert, slot, is_input = row_of((n_send, 1), 0, experts)
    owner = ones_where(expert == iota((n_send, experts), 1))
    copies[0].wait()
    ids = ids_ref[...]
    first = which == ids[0:1, :]
    second = which == ids[1:2, :]
    rank = dot(ones_where(first | second), earlier)
    ranks = jnp.concatenate(
        [jnp.where(first, rank, -1.0), jnp.where(second, rank, -1.0)], axis=1
    ).astype(bf16)
    pick = ones_where(dot(owner, ranks) == slot.astype(f32))
    for copy in copies[1:]:
        copy.wait()
    gates = columns(gates_ref[...])
    cot = cot_ref[...].astype(f32)
    tok = tok_ref[...]
    source = jnp.concatenate(
        [
            jnp.concatenate([tok, (gates[:, 0:1] * cot).astype(bf16)], axis=1),
            jnp.concatenate([tok, (gates[:, 1:2] * cot).astype(bf16)], axis=1),
        ],
        axis=0,
    )
    both = dot(pick, source)
    send_ref[...] = jnp.where(is_input, both[:, :width], both[:, width:]).astype(bf16)


def in_hbm(*arrays):
    return [pltpu.with_memory_space_constraint(a, pltpu.HBM) for a in arrays]


def dispatch(ids, gates, tokens, cotangent, experts):
    rows, width = tokens.shape
    return pl.pallas_call(
        dispatch_kernel,
        in_specs=[pl.BlockSpec(memory_space=pltpu.HBM)] * 4,
        out_shape=jax.ShapeDtypeStruct((2 * experts * CHUNK, width), bf16),
        scratch_shapes=[
            pltpu.VMEM((2, rows), jnp.int32),
            pltpu.VMEM((2, rows), f32),
            pltpu.VMEM((rows, width), bf16),
            pltpu.VMEM((rows, width), bf16),
            pltpu.SemaphoreType.DMA((4,)),
        ],
        compiler_params=pltpu.CompilerParams(vmem_limit_bytes=16 << 20),
        name="dispatch",
    )(*in_hbm(ids.T, gates.T, tokens, cotangent))


def route_kernel(ids_ref, gates_ref, pick_ref, gate_ref):
    rows = ids_ref.shape[1]
    n_send = pick_ref.shape[1]
    experts = n_send // (2 * CHUNK)
    ids = columns(ids_ref[...])
    which = iota((rows, experts), 1)
    first = which == ids[:, 0:1]
    second = which == ids[:, 1:2]
    earlier = ones_where(iota((rows, rows), 1) < iota((rows, rows), 0))
    rank = dot(earlier, ones_where(first | second))
    ranks = jnp.concatenate(
        [jnp.where(first, rank, -1.0), jnp.where(second, rank, -1.0)], axis=0
    ).astype(bf16)
    expert, slot, _ = row_of((1, n_send), 1, experts)
    owner = ones_where(expert == iota((experts, n_send), 0))
    pick_ref[...] = ones_where(dot(ranks, owner) == slot.astype(f32))
    gates = columns(gates_ref[...])
    width = gate_ref.shape[1]
    gate_ref[0:rows, :] = jnp.broadcast_to(gates[:, 0:1], (rows, width))
    gate_ref[rows : 2 * rows, :] = jnp.broadcast_to(gates[:, 1:2], (rows, width))


def route(ids, gates, experts, width):
    rows = ids.shape[0]
    return pl.pallas_call(
        route_kernel,
        out_shape=(
            jax.ShapeDtypeStruct((2 * rows, 2 * experts * CHUNK), bf16),
            jax.ShapeDtypeStruct((2 * rows, width), f32),
        ),
        compiler_params=pltpu.CompilerParams(vmem_limit_bytes=16 << 20),
        name="route",
    )(ids.T, gates.T)


def combine_kernel(pick_ref, gate_ref, ret_ref, out_ref, grad_ref):
    n_send, width = ret_ref.shape
    rows = out_ref.shape[0]
    _, _, is_out = row_of((n_send, 1), 0, n_send // (2 * CHUNK))
    ret = ret_ref[...].astype(f32)
    both = jnp.concatenate(
        [jnp.where(is_out, ret, 0.0), jnp.where(is_out, 0.0, ret)], axis=1
    ).astype(bf16)
    mine = dot(pick_ref[...], both)
    scaled = gate_ref[...] * mine[:, :width]
    out_ref[...] = (scaled[:rows] + scaled[rows:]).astype(bf16)
    grad_ref[...] = (mine[:rows, width:] + mine[rows:, width:]).astype(bf16)


def combine(pick, gate, ret, rows):
    width = ret.shape[-1]
    shape = jax.ShapeDtypeStruct((rows, width), bf16)
    return pl.pallas_call(
        combine_kernel,
        out_shape=(shape, shape),
        compiler_params=pltpu.CompilerParams(vmem_limit_bytes=16 << 20),
        name="combine",
    )(pick, gate, ret)


def expert_kernel(got_ref, win0, wout0, win1, wout1, part_ref, x_hbm, s_hbm, h_hbm, d_hbm, win_ref, wout_ref, x_ref, s_ref, h_ref, d_ref, sems):
    weights = fetch(
        (
            (win0, win_ref.at[0]),
            (win1, win_ref.at[1]),
            (wout0, wout_ref.at[0]),
            (wout1, wout_ref.at[1]),
        ),
        sems,
    )
    n_y, n_rows, width = got_ref.shape
    group = n_rows // 3
    full = group // 2
    half = full // 2
    row, source = iota((half, full), 0), iota((half, full), 1)
    base = (row >> 1) * 4 + (row & 1)
    take_in = ones_where(source == base)
    take_scaled = ones_where(source == base + 2)
    tails = []
    for y in range(n_y):
        for c in range(2):
            at = slice((2 * y + c) * width, (2 * y + c + 1) * width)
            x_ref[0:full, at] = got_ref[y, c * full : (c + 1) * full]
            s_ref[0:full, at] = got_ref[y, 2 * group + c * full : 2 * group + (c + 1) * full]
            tails.append(got_ref[y, group + c * full : group + (c + 1) * full])
    tail = jnp.concatenate(tails, axis=1)
    x_ref[full:, :] = dot(take_in, tail).astype(bf16)
    s_ref[full:, :] = dot(take_scaled, tail).astype(bf16)
    saves = [pltpu.make_async_copy(x_ref, x_hbm, sems.at[4])]
    saves.append(pltpu.make_async_copy(s_ref, s_hbm, sems.at[5]))
    for save in saves:
        save.start()
    out = back = None
    for c in range(2):
        weights[c].wait()
        pre = dot(x_ref[...], win_ref[c])
        cdf = 0.5 * (1.0 + lax.erf(pre * half_root))
        hidden = (pre * cdf).astype(bf16)
        h_ref[c] = hidden
        slope = cdf + pre * inv_root_tau * jnp.exp(-0.5 * pre * pre)
        weights[2 + c].wait()
        d_pre = (dot(s_ref[...], wout_ref[c], 1, 1) * slope).astype(bf16)
        d_ref[c] = d_pre
        for save in (
            pltpu.make_async_copy(h_ref.at[c], h_hbm.at[c], sems.at[6 + c]),
            pltpu.make_async_copy(d_ref.at[c], d_hbm.at[c], sems.at[8 + c]),
        ):
            save.start()
            saves.append(save)
        more, less = dot(hidden, wout_ref[c]), dot(d_pre, win_ref[c], 1, 1)
        out, back = (more, less) if c == 0 else (out + more, back + less)
    out, back = out.astype(bf16), back.astype(bf16)
    tail = dot(take_in, out[full:], 0, 0) + dot(take_scaled, back[full:], 0, 0)
    tail = tail.astype(bf16)
    for y in range(n_y):
        for c in range(2):
            at = slice((2 * y + c) * width, (2 * y + c + 1) * width)
            for k, block in enumerate((out, tail, back)):
                to = k * group + c * full
                part_ref[y, to : to + full] = block[:full, at]
    for save in saves:
        save.wait()


def expert_work(got, w_in, w_out, other_in, other_out):
    n_y, n_rows, width = got.shape
    model, units = w_in.shape
    rows = n_rows // 4
    hbm = pl.BlockSpec(memory_space=pltpu.HBM)
    vmem = pl.BlockSpec(memory_space=pltpu.VMEM)
    feats = pltpu.HBM((rows, model), bf16)
    acts = pltpu.HBM((2, rows, units), bf16)
    return pl.pallas_call(
        expert_kernel,
        in_specs=[vmem] + [hbm] * 4,
        out_specs=[vmem] + [hbm] * 4,
        out_shape=(jax.ShapeDtypeStruct(got.shape, bf16), feats, feats, acts, acts),
        scratch_shapes=[
            pltpu.VMEM((2, model, units), bf16),
            pltpu.VMEM((2, units, model), bf16),
            pltpu.VMEM((rows, model), bf16),
            pltpu.VMEM((rows, model), bf16),
            pltpu.VMEM((2, rows, units), bf16),
            pltpu.VMEM((2, rows, units), bf16),
            pltpu.SemaphoreType.DMA((10,)),
        ],
        compiler_params=pltpu.CompilerParams(vmem_limit_bytes=32 << 20),
        name="expert",
    )(got, *in_hbm(w_in, w_out, other_in, other_out))


def fold_kernel(parts_ref, out_ref):
    parts = [parts_ref[y].astype(f32) for y in range(parts_ref.shape[0])]
    out_ref[...] = sum(parts[1:], parts[0]).astype(bf16)


def fold(parts):
    return pl.pallas_call(
        fold_kernel,
        out_shape=jax.ShapeDtypeStruct(parts.shape[1:], bf16),
        compiler_params=pltpu.CompilerParams(vmem_limit_bytes=12 << 20),
        name="fold",
    )(parts)


def on_device(tokens, cotangent, expert_ids, gate_weights, weight_in, weight_out):
    experts = lax.axis_size("x") * lax.axis_size("z")
    n_y = lax.axis_size("y")
    rows, width = tokens.shape
    swap = [(0, 1), (1, 0)]
    w_in, w_out = weight_in[0], weight_out[0]
    send = dispatch(expert_ids, gate_weights, tokens, cotangent, experts)
    chunks = (2 * experts, CHUNK // 4, 4, width)
    with jax.named_scope("to_experts"):
        got = lax.all_to_all(send.reshape(chunks), CXZ, 0, 0, tiled=True)
    with jax.named_scope("weights"):
        other_in = lax.ppermute(w_in, "core", swap)
        other_out = lax.ppermute(w_out, "core", swap)
    got = jnp.transpose(got, (1, 0, 2, 3)).reshape(1, -1, width)
    got = jnp.broadcast_to(got, (n_y,) + got.shape[1:])
    got = lax.all_to_all(got, "y", 0, 0, tiled=True)
    part, x, s, h, d = expert_work(got, w_in, w_out, other_in, other_out)
    summed = fold(lax.all_to_all(part, "y", 0, 0, tiled=True))
    summed = jnp.transpose(summed.reshape(chunks[1], chunks[0], 4, width), (1, 0, 2, 3))
    summed, ids, gates = lax.optimization_barrier((summed, expert_ids, gate_weights))
    pick, gate = route(ids, gates, experts, width)
    ret = lax.all_to_all(summed, CXZ, 0, 0, tiled=True).reshape(-1, width)
    output, grad_tokens = combine(pick, gate, ret, rows)
    their_out = lax.ppermute(dot(h[1], s, 0, 0).astype(bf16), "core", swap)
    their_in = lax.ppermute(dot(x, d[1], 0, 0).astype(bf16), "core", swap)
    grad_out = (dot(h[0], s, 0, 0) + their_out.astype(f32)).astype(bf16)
    grad_in = (dot(x, d[0], 0, 0) + their_in.astype(f32)).astype(bf16)
    return output, grad_tokens, grad_in[None], grad_out[None]


def solution(mesh):
    cores = 2
    n_dp, n_expert = mesh.devices.shape
    n_x = 4
    grid = mesh.devices.reshape(n_dp // cores, cores, n_x, n_expert // n_x)
    fine = Mesh(grid, ("y", "core", "x", "z"))
    dp = ("y", "core")
    return jax.shard_map(
        on_device,
        mesh=fine,
        in_specs=(P(XZ, dp), P(XZ, dp), P(XZ, None), P(XZ, None), P(XZ, None, dp), P(XZ, dp, None)),
        out_specs=(P(XZ, dp), P(XZ, dp), P(XZ, None, dp), P(XZ, dp, None)),
        check_vma=False,
    )
```

```python
import jax
import jax.numpy as jnp
from jax import lax
from jax.experimental import pallas as pl
from jax.experimental.pallas import tpu as pltpu
from jax.sharding import Mesh, PartitionSpec as P

half_root = 0.7071067811865476
inv_root_tau = 0.3989422804014327

XZ = ("x", "z")
CXZ = ("core", "x", "z")
bf16 = jnp.bfloat16
f32 = jnp.float32

HALF = 6
CHUNK = 12


def dot(left, right, left_dim=1, right_dim=0):
    return lax.dot_general(
        left, right, (((left_dim,), (right_dim,)), ((), ())), preferred_element_type=f32
    )


def iota(shape, dim):
    return lax.broadcasted_iota(jnp.int32, shape, dim)


def columns(rows):
    pad = jnp.zeros((8 - rows.shape[0], rows.shape[1]), rows.dtype)
    return jnp.transpose(jnp.concatenate([rows, pad], axis=0))


def ones_where(mask):
    return jnp.where(mask, 1.0, 0.0).astype(bf16)


def fetch(pairs, sems):
    copies = [pltpu.make_async_copy(src, dst, sems.at[i]) for i, (src, dst) in enumerate(pairs)]
    for copy in copies:
        copy.start()
    return copies


def row_of(shape, dim, experts):
    row = iota(shape, dim)
    chunk = ((row.astype(f32) + 0.5) * (1.0 / CHUNK)).astype(jnp.int32)
    at = row - CHUNK * chunk
    core = jnp.where(chunk >= experts, 1, 0)
    group, place = at >> 2, at & 3
    mixed = group == 1
    is_input = jnp.where(mixed, place >> 1, group) == 0
    slot = HALF * core + jnp.where(mixed, 4 + (place & 1), place)
    return chunk - experts * core, slot, is_input


def dispatch_kernel(ids_hbm, gates_hbm, tok_hbm, cot_hbm, send_ref, ids_ref, gates_ref, tok_ref, cot_ref, sems):
    copies = fetch(
        ((ids_hbm, ids_ref), (gates_hbm, gates_ref), (tok_hbm, tok_ref), (cot_hbm, cot_ref)), sems
    )
    n_send, width = send_ref.shape
    experts = n_send // (2 * CHUNK)
    rows = tok_ref.shape[0]
    which = iota((experts, rows), 0)
    earlier = ones_where(iota((rows, rows), 0) < iota((rows, rows), 1))
    expert, slot, is_input = row_of((n_send, 1), 0, experts)
    owner = ones_where(expert == iota((n_send, experts), 1))
    copies[0].wait()
    ids = ids_ref[...]
    first = which == ids[0:1, :]
    second = which == ids[1:2, :]
    rank = dot(ones_where(first | second), earlier)
    ranks = jnp.concatenate(
        [jnp.where(first, rank, -1.0), jnp.where(second, rank, -1.0)], axis=1
    ).astype(bf16)
    pick = ones_where(dot(owner, ranks) == slot.astype(f32))
    for copy in copies[1:]:
        copy.wait()
    gates = columns(gates_ref[...])
    cot = cot_ref[...].astype(f32)
    tok = tok_ref[...]
    source = jnp.concatenate(
        [
            jnp.concatenate([tok, (gates[:, 0:1] * cot).astype(bf16)], axis=1),
            jnp.concatenate([tok, (gates[:, 1:2] * cot).astype(bf16)], axis=1),
        ],
        axis=0,
    )
    both = dot(pick, source)
    send_ref[...] = jnp.where(is_input, both[:, :width], both[:, width:]).astype(bf16)


def in_hbm(*arrays):
    return [pltpu.with_memory_space_constraint(a, pltpu.HBM) for a in arrays]


def dispatch(ids, gates, tokens, cotangent, experts):
    rows, width = tokens.shape
    return pl.pallas_call(
        dispatch_kernel,
        in_specs=[pl.BlockSpec(memory_space=pltpu.HBM)] * 4,
        out_shape=jax.ShapeDtypeStruct((2 * experts * CHUNK, width), bf16),
        scratch_shapes=[
            pltpu.VMEM((2, rows), jnp.int32),
            pltpu.VMEM((2, rows), f32),
            pltpu.VMEM((rows, width), bf16),
            pltpu.VMEM((rows, width), bf16),
            pltpu.SemaphoreType.DMA((4,)),
        ],
        compiler_params=pltpu.CompilerParams(vmem_limit_bytes=16 << 20),
        name="dispatch",
    )(*in_hbm(ids.T, gates.T, tokens, cotangent))


def route_kernel(ids_ref, gates_ref, pick_ref, gate_ref):
    rows = ids_ref.shape[1]
    n_send = pick_ref.shape[1]
    experts = n_send // (2 * CHUNK)
    ids = columns(ids_ref[...])
    which = iota((rows, experts), 1)
    first = which == ids[:, 0:1]
    second = which == ids[:, 1:2]
    earlier = ones_where(iota((rows, rows), 1) < iota((rows, rows), 0))
    rank = dot(earlier, ones_where(first | second))
    ranks = jnp.concatenate(
        [jnp.where(first, rank, -1.0), jnp.where(second, rank, -1.0)], axis=0
    ).astype(bf16)
    expert, slot, _ = row_of((1, n_send), 1, experts)
    owner = ones_where(expert == iota((experts, n_send), 0))
    pick_ref[...] = ones_where(dot(ranks, owner) == slot.astype(f32))
    gates = columns(gates_ref[...])
    width = gate_ref.shape[1]
    gate_ref[0:rows, :] = jnp.broadcast_to(gates[:, 0:1], (rows, width))
    gate_ref[rows : 2 * rows, :] = jnp.broadcast_to(gates[:, 1:2], (rows, width))


def route(ids, gates, experts, width):
    rows = ids.shape[0]
    return pl.pallas_call(
        route_kernel,
        out_shape=(
            jax.ShapeDtypeStruct((2 * rows, 2 * experts * CHUNK), bf16),
            jax.ShapeDtypeStruct((2 * rows, width), f32),
        ),
        compiler_params=pltpu.CompilerParams(vmem_limit_bytes=16 << 20),
        name="route",
    )(ids.T, gates.T)


def combine_kernel(pick_ref, gate_ref, ret_ref, out_ref, grad_ref):
    n_send, width = ret_ref.shape
    rows = out_ref.shape[0]
    _, _, is_out = row_of((n_send, 1), 0, n_send // (2 * CHUNK))
    ret = ret_ref[...].astype(f32)
    both = jnp.concatenate(
        [jnp.where(is_out, ret, 0.0), jnp.where(is_out, 0.0, ret)], axis=1
    ).astype(bf16)
    mine = dot(pick_ref[...], both)
    scaled = gate_ref[...] * mine[:, :width]
    out_ref[...] = (scaled[:rows] + scaled[rows:]).astype(bf16)
    grad_ref[...] = (mine[:rows, width:] + mine[rows:, width:]).astype(bf16)


def combine(pick, gate, ret, rows):
    width = ret.shape[-1]
    shape = jax.ShapeDtypeStruct((rows, width), bf16)
    return pl.pallas_call(
        combine_kernel,
        out_shape=(shape, shape),
        compiler_params=pltpu.CompilerParams(vmem_limit_bytes=16 << 20),
        name="combine",
    )(pick, gate, ret)


def expert_kernel(got_ref, win0, wout0, win1, wout1, part_ref, x_hbm, s_hbm, h_hbm, d_hbm, win_ref, wout_ref, x_ref, s_ref, h_ref, d_ref, sems):
    weights = fetch(
        (
            (win0, win_ref.at[0]),
            (win1, win_ref.at[1]),
            (wout0, wout_ref.at[0]),
            (wout1, wout_ref.at[1]),
        ),
        sems,
    )
    n_y, n_rows, width = got_ref.shape
    group = n_rows // 3
    full = group // 2
    half = full // 2
    row, source = iota((half, full), 0), iota((half, full), 1)
    base = (row >> 1) * 4 + (row & 1)
    take_in = ones_where(source == base)
    take_scaled = ones_where(source == base + 2)
    tails = []
    for y in range(n_y):
        for c in range(2):
            at = slice((2 * y + c) * width, (2 * y + c + 1) * width)
            x_ref[0:full, at] = got_ref[y, c * full : (c + 1) * full]
            s_ref[0:full, at] = got_ref[y, 2 * group + c * full : 2 * group + (c + 1) * full]
            tails.append(got_ref[y, group + c * full : group + (c + 1) * full])
    tail = jnp.concatenate(tails, axis=1)
    x_ref[full:, :] = dot(take_in, tail).astype(bf16)
    s_ref[full:, :] = dot(take_scaled, tail).astype(bf16)
    saves = [pltpu.make_async_copy(x_ref, x_hbm, sems.at[4])]
    saves.append(pltpu.make_async_copy(s_ref, s_hbm, sems.at[5]))
    for save in saves:
        save.start()
    out = back = None
    for c in range(2):
        weights[c].wait()
        pre = dot(x_ref[...], win_ref[c])
        cdf = 0.5 * (1.0 + lax.erf(pre * half_root))
        hidden = (pre * cdf).astype(bf16)
        h_ref[c] = hidden
        slope = cdf + pre * inv_root_tau * jnp.exp(-0.5 * pre * pre)
        weights[2 + c].wait()
        d_pre = (dot(s_ref[...], wout_ref[c], 1, 1) * slope).astype(bf16)
        d_ref[c] = d_pre
        for save in (
            pltpu.make_async_copy(h_ref.at[c], h_hbm.at[c], sems.at[6 + c]),
            pltpu.make_async_copy(d_ref.at[c], d_hbm.at[c], sems.at[8 + c]),
        ):
            save.start()
            saves.append(save)
        more, less = dot(hidden, wout_ref[c]), dot(d_pre, win_ref[c], 1, 1)
        out, back = (more, less) if c == 0 else (out + more, back + less)
    out, back = out.astype(bf16), back.astype(bf16)
    tail = dot(take_in, out[full:], 0, 0) + dot(take_scaled, back[full:], 0, 0)
    tail = tail.astype(bf16)
    for y in range(n_y):
        for c in range(2):
            at = slice((2 * y + c) * width, (2 * y + c + 1) * width)
            for k, block in enumerate((out, tail, back)):
                to = k * group + c * full
                part_ref[y, to : to + full] = block[:full, at]
    for save in saves:
        save.wait()


def expert_work(got, w_in, w_out, other_in, other_out):
    n_y, n_rows, width = got.shape
    model, units = w_in.shape
    rows = n_rows // 4
    hbm = pl.BlockSpec(memory_space=pltpu.HBM)
    vmem = pl.BlockSpec(memory_space=pltpu.VMEM)
    feats = pltpu.HBM((rows, model), bf16)
    acts = pltpu.HBM((2, rows, units), bf16)
    return pl.pallas_call(
        expert_kernel,
        in_specs=[vmem] + [hbm] * 4,
        out_specs=[vmem] + [hbm] * 4,
        out_shape=(jax.ShapeDtypeStruct(got.shape, bf16), feats, feats, acts, acts),
        scratch_shapes=[
            pltpu.VMEM((2, model, units), bf16),
            pltpu.VMEM((2, units, model), bf16),
            pltpu.VMEM((rows, model), bf16),
            pltpu.VMEM((rows, model), bf16),
            pltpu.VMEM((2, rows, units), bf16),
            pltpu.VMEM((2, rows, units), bf16),
            pltpu.SemaphoreType.DMA((10,)),
        ],
        compiler_params=pltpu.CompilerParams(vmem_limit_bytes=32 << 20),
        name="expert",
    )(got, *in_hbm(w_in, w_out, other_in, other_out))


def fold_kernel(parts_ref, out_ref):
    parts = [parts_ref[y].astype(f32) for y in range(parts_ref.shape[0])]
    out_ref[...] = sum(parts[1:], parts[0]).astype(bf16)


def fold(parts):
    return pl.pallas_call(
        fold_kernel,
        out_shape=jax.ShapeDtypeStruct(parts.shape[1:], bf16),
        compiler_params=pltpu.CompilerParams(vmem_limit_bytes=12 << 20),
        name="fold",
    )(parts)


def on_device(tokens, cotangent, expert_ids, gate_weights, weight_in, weight_out):
    experts = lax.axis_size("x") * lax.axis_size("z")
    n_y = lax.axis_size("y")
    rows, width = tokens.shape
    swap = [(0, 1), (1, 0)]
    w_in, w_out = weight_in[0], weight_out[0]
    send = dispatch(expert_ids, gate_weights, tokens, cotangent, experts)
    chunks = (2 * experts, CHUNK // 4, 4, width)
    with jax.named_scope("to_experts"):
        got = lax.all_to_all(send.reshape(chunks), CXZ, 0, 0, tiled=True)
    with jax.named_scope("weights"):
        other_in = lax.ppermute(w_in, "core", swap)
        other_out = lax.ppermute(w_out, "core", swap)
    got, other_in, other_out = lax.optimization_barrier((got, other_in, other_out))
    got = jnp.transpose(got, (1, 0, 2, 3)).reshape(1, -1, width)
    got = jnp.broadcast_to(got, (n_y,) + got.shape[1:])
    got = lax.all_to_all(got, "y", 0, 0, tiled=True)
    part, x, s, h, d = expert_work(got, w_in, w_out, other_in, other_out)
    summed = fold(lax.all_to_all(part, "y", 0, 0, tiled=True))
    summed = jnp.transpose(summed.reshape(chunks[1], chunks[0], 4, width), (1, 0, 2, 3))
    summed, ids, gates, x, s, h, d = lax.optimization_barrier(
        (summed, expert_ids, gate_weights, x, s, h, d)
    )
    pick, gate = route(ids, gates, experts, width)
    ret = lax.all_to_all(summed, CXZ, 0, 0, tiled=True).reshape(-1, width)
    output, grad_tokens = combine(pick, gate, ret, rows)
    their_out = lax.ppermute(dot(h[1], s, 0, 0).astype(bf16), "core", swap)
    their_in = lax.ppermute(dot(x, d[1], 0, 0).astype(bf16), "core", swap)
    grad_out = (dot(h[0], s, 0, 0) + their_out.astype(f32)).astype(bf16)
    grad_in = (dot(x, d[0], 0, 0) + their_in.astype(f32)).astype(bf16)
    return output, grad_tokens, grad_in[None], grad_out[None]


def solution(mesh):
    cores = 2
    n_dp, n_expert = mesh.devices.shape
    n_x = 4
    grid = mesh.devices.reshape(n_dp // cores, cores, n_x, n_expert // n_x)
    fine = Mesh(grid, ("y", "core", "x", "z"))
    dp = ("y", "core")
    return jax.shard_map(
        on_device,
        mesh=fine,
        in_specs=(P(XZ, dp), P(XZ, dp), P(XZ, None), P(XZ, None), P(XZ, None, dp), P(XZ, dp, None)),
        out_specs=(P(XZ, dp), P(XZ, dp), P(XZ, None, dp), P(XZ, dp, None)),
        check_vma=False,
    )
```

```python
import jax
import jax.numpy as jnp
from jax import lax
from jax.experimental import pallas as pl
from jax.experimental.pallas import tpu as pltpu
from jax.sharding import Mesh, PartitionSpec as P

half_root = 0.7071067811865476
inv_root_tau = 0.3989422804014327

XZ = ("x", "z")
CXZ = ("core", "x", "z")
bf16 = jnp.bfloat16
f32 = jnp.float32

HALF = 6
CHUNK = 12


def dot(left, right, left_dim=1, right_dim=0):
    return lax.dot_general(
        left, right, (((left_dim,), (right_dim,)), ((), ())), preferred_element_type=f32
    )


def iota(shape, dim):
    return lax.broadcasted_iota(jnp.int32, shape, dim)


def columns(rows):
    pad = jnp.zeros((8 - rows.shape[0], rows.shape[1]), rows.dtype)
    return jnp.transpose(jnp.concatenate([rows, pad], axis=0))


def ones_where(mask):
    return jnp.where(mask, 1.0, 0.0).astype(bf16)


def fetch(pairs, sems):
    copies = [pltpu.make_async_copy(src, dst, sems.at[i]) for i, (src, dst) in enumerate(pairs)]
    for copy in copies:
        copy.start()
    return copies


def row_of(shape, dim, experts):
    row = iota(shape, dim)
    chunk = ((row.astype(f32) + 0.5) * (1.0 / CHUNK)).astype(jnp.int32)
    at = row - CHUNK * chunk
    core = jnp.where(chunk >= experts, 1, 0)
    group, place = at >> 2, at & 3
    mixed = group == 1
    is_input = jnp.where(mixed, place >> 1, group) == 0
    slot = HALF * core + jnp.where(mixed, 4 + (place & 1), place)
    return chunk - experts * core, slot, is_input


def dispatch_kernel(ids_hbm, gates_hbm, tok_hbm, cot_hbm, send_hbm, ids_ref, gates_ref, tok_ref, cot_ref, send_ref, sems, out_sems):
    writes, parts = [], out_sems.shape[0]
    copies = fetch(
        ((ids_hbm, ids_ref), (gates_hbm, gates_ref), (tok_hbm, tok_ref), (cot_hbm, cot_ref)), sems
    )
    n_send, width = send_ref.shape
    experts = n_send // (2 * CHUNK)
    rows = tok_ref.shape[0]
    which = iota((experts, rows), 0)
    earlier = ones_where(iota((rows, rows), 0) < iota((rows, rows), 1))
    expert, slot, is_input = row_of((n_send, 1), 0, experts)
    owner = ones_where(expert == iota((n_send, experts), 1))
    copies[0].wait()
    ids = ids_ref[...]
    first = which == ids[0:1, :]
    second = which == ids[1:2, :]
    rank = dot(ones_where(first | second), earlier)
    ranks = jnp.concatenate(
        [jnp.where(first, rank, -1.0), jnp.where(second, rank, -1.0)], axis=1
    ).astype(bf16)
    for copy in copies[1:]:
        copy.wait()
    gates = columns(gates_ref[...])
    cot = cot_ref[...].astype(f32)
    tok = tok_ref[...]
    source = jnp.concatenate(
        [
            jnp.concatenate([tok, (gates[:, 0:1] * cot).astype(bf16)], axis=1),
            jnp.concatenate([tok, (gates[:, 1:2] * cot).astype(bf16)], axis=1),
        ],
        axis=0,
    )
    slot = slot.astype(f32)
    step = n_send // parts
    for i in range(parts):
        at = slice(i * step, (i + 1) * step)
        both = dot(ones_where(dot(owner[at], ranks) == slot[at]), source)
        send_ref[at] = jnp.where(is_input[at], both[:, :width], both[:, width:]).astype(bf16)
        write = pltpu.make_async_copy(send_ref.at[at], send_hbm.at[at], out_sems.at[i])
        write.start()
        writes.append(write)
    for write in writes:
        write.wait()


def in_hbm(*arrays):
    return [pltpu.with_memory_space_constraint(a, pltpu.HBM) for a in arrays]


def dispatch(ids, gates, tokens, cotangent, experts):
    rows, width = tokens.shape
    return pl.pallas_call(
        dispatch_kernel,
        in_specs=[pl.BlockSpec(memory_space=pltpu.HBM)] * 4,
        out_specs=pl.BlockSpec(memory_space=pltpu.HBM),
        out_shape=pltpu.HBM((2 * experts * CHUNK, width), bf16),
        scratch_shapes=[
            pltpu.VMEM((2, rows), jnp.int32),
            pltpu.VMEM((2, rows), f32),
            pltpu.VMEM((rows, width), bf16),
            pltpu.VMEM((rows, width), bf16),
            pltpu.VMEM((2 * experts * CHUNK, width), bf16),
            pltpu.SemaphoreType.DMA((4,)),
            pltpu.SemaphoreType.DMA((4,)),
        ],
        compiler_params=pltpu.CompilerParams(vmem_limit_bytes=16 << 20),
        name="dispatch",
    )(*in_hbm(ids.T, gates.T, tokens, cotangent))


def route_kernel(ids_ref, gates_ref, pick_ref, gate_ref):
    rows = ids_ref.shape[1]
    n_send = pick_ref.shape[1]
    experts = n_send // (2 * CHUNK)
    ids = columns(ids_ref[...])
    which = iota((rows, experts), 1)
    first = which == ids[:, 0:1]
    second = which == ids[:, 1:2]
    earlier = ones_where(iota((rows, rows), 1) < iota((rows, rows), 0))
    rank = dot(earlier, ones_where(first | second))
    ranks = jnp.concatenate(
        [jnp.where(first, rank, -1.0), jnp.where(second, rank, -1.0)], axis=0
    ).astype(bf16)
    expert, slot, _ = row_of((1, n_send), 1, experts)
    owner = ones_where(expert == iota((experts, n_send), 0))
    pick_ref[...] = ones_where(dot(ranks, owner) == slot.astype(f32))
    gates = columns(gates_ref[...])
    width = gate_ref.shape[1]
    gate_ref[0:rows, :] = jnp.broadcast_to(gates[:, 0:1], (rows, width))
    gate_ref[rows : 2 * rows, :] = jnp.broadcast_to(gates[:, 1:2], (rows, width))


def route(ids, gates, experts, width):
    rows = ids.shape[0]
    return pl.pallas_call(
        route_kernel,
        out_shape=(
            jax.ShapeDtypeStruct((2 * rows, 2 * experts * CHUNK), bf16),
            jax.ShapeDtypeStruct((2 * rows, width), f32),
        ),
        compiler_params=pltpu.CompilerParams(vmem_limit_bytes=16 << 20),
        name="route",
    )(ids.T, gates.T)


def combine_kernel(pick_ref, gate_ref, ret_ref, out_ref, grad_ref):
    n_send, width = ret_ref.shape
    rows = out_ref.shape[0]
    _, _, is_out = row_of((n_send, 1), 0, n_send // (2 * CHUNK))
    ret = ret_ref[...].astype(f32)
    both = jnp.concatenate(
        [jnp.where(is_out, ret, 0.0), jnp.where(is_out, 0.0, ret)], axis=1
    ).astype(bf16)
    mine = dot(pick_ref[...], both)
    scaled = gate_ref[...] * mine[:, :width]
    out_ref[...] = (scaled[:rows] + scaled[rows:]).astype(bf16)
    grad_ref[...] = (mine[:rows, width:] + mine[rows:, width:]).astype(bf16)


def combine(pick, gate, ret, rows):
    width = ret.shape[-1]
    shape = jax.ShapeDtypeStruct((rows, width), bf16)
    return pl.pallas_call(
        combine_kernel,
        out_shape=(shape, shape),
        compiler_params=pltpu.CompilerParams(vmem_limit_bytes=16 << 20),
        name="combine",
    )(pick, gate, ret)


def expert_kernel(got_ref, win0, wout0, win1, wout1, part_ref, x_hbm, s_hbm, h_hbm, d_hbm, win_ref, wout_ref, x_ref, s_ref, h_ref, d_ref, sems):
    weights = fetch(((win0, win_ref.at[0]), (wout0, wout_ref.at[0])), sems)
    later = (
        pltpu.make_async_copy(win1, win_ref.at[1], sems.at[2]),
        pltpu.make_async_copy(wout1, wout_ref.at[1], sems.at[3]),
    )
    n_y, n_rows, width = got_ref.shape
    group = n_rows // 3
    full = group // 2
    half = full // 2
    row, source = iota((half, full), 0), iota((half, full), 1)
    base = (row >> 1) * 4 + (row & 1)
    take_in = ones_where(source == base)
    take_scaled = ones_where(source == base + 2)
    tails = []
    for y in range(n_y):
        for c in range(2):
            at = slice((2 * y + c) * width, (2 * y + c + 1) * width)
            x_ref[0:full, at] = got_ref[y, c * full : (c + 1) * full]
            s_ref[0:full, at] = got_ref[y, 2 * group + c * full : 2 * group + (c + 1) * full]
            tails.append(got_ref[y, group + c * full : group + (c + 1) * full])
    tail = jnp.concatenate(tails, axis=1)
    x_ref[full:, :] = dot(take_in, tail).astype(bf16)
    s_ref[full:, :] = dot(take_scaled, tail).astype(bf16)
    saves = [pltpu.make_async_copy(x_ref, x_hbm, sems.at[4])]
    saves.append(pltpu.make_async_copy(s_ref, s_hbm, sems.at[5]))
    for save in saves:
        save.start()
    out = back = None
    for c in range(2):
        (weights[0] if c == 0 else later[0]).wait()
        if c == 0:
            for copy in later:
                copy.start()
        pre = dot(x_ref[...], win_ref[c])
        cdf = 0.5 * (1.0 + lax.erf(pre * half_root))
        hidden = (pre * cdf).astype(bf16)
        h_ref[c] = hidden
        slope = cdf + pre * inv_root_tau * jnp.exp(-0.5 * pre * pre)
        (weights[1] if c == 0 else later[1]).wait()
        d_pre = (dot(s_ref[...], wout_ref[c], 1, 1) * slope).astype(bf16)
        d_ref[c] = d_pre
        for save in (
            pltpu.make_async_copy(h_ref.at[c], h_hbm.at[c], sems.at[6 + c]),
            pltpu.make_async_copy(d_ref.at[c], d_hbm.at[c], sems.at[8 + c]),
        ):
            save.start()
            saves.append(save)
        more, less = dot(hidden, wout_ref[c]), dot(d_pre, win_ref[c], 1, 1)
        out, back = (more, less) if c == 0 else (out + more, back + less)
    out, back = out.astype(bf16), back.astype(bf16)
    tail = dot(take_in, out[full:], 0, 0) + dot(take_scaled, back[full:], 0, 0)
    tail = tail.astype(bf16)
    for y in range(n_y):
        for c in range(2):
            at = slice((2 * y + c) * width, (2 * y + c + 1) * width)
            for k, block in enumerate((out, tail, back)):
                to = k * group + c * full
                part_ref[y, to : to + full] = block[:full, at]
    for save in saves:
        save.wait()


def expert_work(got, w_in, w_out, other_in, other_out):
    n_y, n_rows, width = got.shape
    model, units = w_in.shape
    rows = n_rows // 4
    hbm = pl.BlockSpec(memory_space=pltpu.HBM)
    vmem = pl.BlockSpec(memory_space=pltpu.VMEM)
    feats = pltpu.HBM((rows, model), bf16)
    acts = pltpu.HBM((2, rows, units), bf16)
    return pl.pallas_call(
        expert_kernel,
        in_specs=[vmem] + [hbm] * 4,
        out_specs=[vmem] + [hbm] * 4,
        out_shape=(jax.ShapeDtypeStruct(got.shape, bf16), feats, feats, acts, acts),
        scratch_shapes=[
            pltpu.VMEM((2, model, units), bf16),
            pltpu.VMEM((2, units, model), bf16),
            pltpu.VMEM((rows, model), bf16),
            pltpu.VMEM((rows, model), bf16),
            pltpu.VMEM((2, rows, units), bf16),
            pltpu.VMEM((2, rows, units), bf16),
            pltpu.SemaphoreType.DMA((10,)),
        ],
        compiler_params=pltpu.CompilerParams(vmem_limit_bytes=32 << 20),
        name="expert",
    )(got, *in_hbm(w_in, w_out, other_in, other_out))


def fold_kernel(parts_ref, out_hbm, sum_ref, sems):
    n_y, n_rows, width = parts_ref.shape
    step = n_rows // 3
    writes = []
    for k in range(3):
        at = slice(k * step, (k + 1) * step)
        parts = [parts_ref[y, at].astype(f32) for y in range(n_y)]
        sum_ref[k] = sum(parts[1:], parts[0]).reshape(step // 4, 4, width).astype(bf16)
        write = pltpu.make_async_copy(sum_ref.at[k], out_hbm.at[:, k], sems.at[k])
        write.start()
        writes.append(write)
    for write in writes:
        write.wait()


def fold(parts):
    _, n_rows, width = parts.shape
    return pl.pallas_call(
        fold_kernel,
        out_specs=pl.BlockSpec(memory_space=pltpu.HBM),
        out_shape=pltpu.HBM((n_rows // CHUNK, 3, 4, width), bf16),
        scratch_shapes=[
            pltpu.VMEM((3, n_rows // CHUNK, 4, width), bf16),
            pltpu.SemaphoreType.DMA((3,)),
        ],
        compiler_params=pltpu.CompilerParams(vmem_limit_bytes=12 << 20),
        name="fold",
    )(parts)


def on_device(tokens, cotangent, expert_ids, gate_weights, weight_in, weight_out):
    experts = lax.axis_size("x") * lax.axis_size("z")
    n_y = lax.axis_size("y")
    rows, width = tokens.shape
    swap = [(0, 1), (1, 0)]
    w_in, w_out = weight_in[0], weight_out[0]
    send = dispatch(expert_ids, gate_weights, tokens, cotangent, experts)
    chunks = (2 * experts, CHUNK // 4, 4, width)
    with jax.named_scope("to_experts"):
        got = lax.all_to_all(send.reshape(chunks), CXZ, 0, 0, tiled=True)
    with jax.named_scope("weights"):
        other_in = lax.ppermute(w_in, "core", swap)
        other_out = lax.ppermute(w_out, "core", swap)
    got, other_in, other_out = lax.optimization_barrier((got, other_in, other_out))
    got = jnp.transpose(got, (1, 0, 2, 3)).reshape(1, -1, width)
    got = jnp.broadcast_to(got, (n_y,) + got.shape[1:])
    got = lax.all_to_all(got, "y", 0, 0, tiled=True)
    part, x, s, h, d = expert_work(got, w_in, w_out, other_in, other_out)
    summed = fold(lax.all_to_all(part, "y", 0, 0, tiled=True))
    summed, ids, gates, x, s, h, d = lax.optimization_barrier(
        (summed, expert_ids, gate_weights, x, s, h, d)
    )
    pick, gate = route(ids, gates, experts, width)
    ret = lax.all_to_all(summed, CXZ, 0, 0, tiled=True).reshape(-1, width)
    output, grad_tokens = combine(pick, gate, ret, rows)
    their_out = lax.ppermute(dot(h[1], s, 0, 0).astype(bf16), "core", swap)
    their_in = lax.ppermute(dot(x, d[1], 0, 0).astype(bf16), "core", swap)
    grad_out = (dot(h[0], s, 0, 0) + their_out.astype(f32)).astype(bf16)
    grad_in = (dot(x, d[0], 0, 0) + their_in.astype(f32)).astype(bf16)
    return output, grad_tokens, grad_in[None], grad_out[None]


def solution(mesh):
    cores = 2
    n_dp, n_expert = mesh.devices.shape
    n_x = 4
    grid = mesh.devices.reshape(n_dp // cores, cores, n_x, n_expert // n_x)
    fine = Mesh(grid, ("y", "core", "x", "z"))
    dp = ("y", "core")
    return jax.shard_map(
        on_device,
        mesh=fine,
        in_specs=(P(XZ, dp), P(XZ, dp), P(XZ, None), P(XZ, None), P(XZ, None, dp), P(XZ, dp, None)),
        out_specs=(P(XZ, dp), P(XZ, dp), P(XZ, None, dp), P(XZ, dp, None)),
        check_vma=False,
    )
```
